256 devices in a mesh: col: 8 (over y, x_hi), row: 32 (over z, x_lo, core).
Axes of the slice: x: 4 (x_hi: 2, x_lo: 2; x = x_hi * 2 + x_lo), y: 4, z: 8, core: 2. Of those that a mesh axis runs over, the one named last changes fastest.
Arguments:
- weights: float32 [16384, 16384], P('row', 'col'), may hold values from -6 to 6
- factor_rows: bfloat16 [1024, 16384], P('row', 'col'), may hold values from -0.25 to 0.25
- diag_inverse: bfloat16 [8, 128, 128], replicated, as said below
- prune_tiles: int32 [128, 8], P('row'), may hold values 0 or 1
- pivot_order: int32 [8], replicated, may hold values from 0 to 127, as said below
Outputs:
- pruned_weights: float32 [16384, 16384], P('row', 'col')
The draws below stay inside these ranges and needn't reach their ends.
Inputs may be any that keep to these rules, and one draw needn't show every extreme that they name: `pivot_order`: the 8 block numbers are distinct; block 0 and the last block are among them. `diag_inverse`: each block is upper triangular with positive diagonal.
All inputs are finite; a program needn't handle non-finite values. No bound on the sum of `prune_tiles` on one device may be relied on, other than what follows from the above.
Results may differ from the reference program's by a relative error of at most 0.0003.
Values may be sent and summed in bfloat16 or wider, within the bound.
A program may use at most 64 MiB of HBM per device.

```python
import jax
import jax.numpy as jnp
from jax import lax

ROWS = 16384
COLS = 16384
BLOCK = 128
PIVOTS = 8


def draw_pivot_order(key, part):
    nblocks = COLS // BLOCK
    first, second = jax.random.split(jax.random.fold_in(key, 29))
    middle = jax.random.permutation(first, nblocks - 2)[:PIVOTS - 2].astype(jnp.int32) + 1
    chosen = jnp.concatenate([jnp.zeros((1,), jnp.int32), jnp.full((1,), nblocks - 1, jnp.int32), middle])
    return jax.random.permutation(second, chosen).astype(jnp.int32)


def draw_diag_inverse(key, part):
    first, second = jax.random.split(jax.random.fold_in(key, 17))
    diagonal = jnp.exp(jax.random.uniform(first, (PIVOTS, BLOCK), jnp.float32, jnp.log(0.5), jnp.log(2.0)))
    offdiag = 0.5 * jax.random.normal(second, (PIVOTS, BLOCK, BLOCK), jnp.float32) / jnp.sqrt(jnp.float32(BLOCK))
    upper = jnp.triu(offdiag, 1) + diagonal[:, :, None] * jnp.eye(BLOCK, dtype=jnp.float32)[None]
    return upper.astype(jnp.bfloat16)


def place_ends(result, key, least, high):
    place = [jax.random.randint(jax.random.fold_in(key, axis), (), 0, length) for axis, length in enumerate(result.shape)]
    longest = result.shape.index(max(result.shape))
    beside = place[:longest] + [(place[longest] + 1) % result.shape[longest]] + place[longest + 1:]
    return result.at[tuple(place)].set(least).at[tuple(beside)].set(high)


def steps_of(key, dims, shards, least, top_value):
    gain = 1.0
    for axis_at, blocks in shards:
        heights = jax.random.uniform(jax.random.fold_in(jax.random.fold_in(key, 6), axis_at), (blocks,), jnp.float32, least / len(shards), top_value / len(shards))
        gain = gain * jnp.repeat(jnp.exp(heights), dims[axis_at] // blocks).reshape((-1,) + (1,) * (len(dims) - 1 - axis_at))
    return gain


def bell_draw(own_key, shape, width, reach, shards=(), kind=jnp.bfloat16):
    drawn = jax.random.normal(own_key, shape, jnp.float32) * width
    if len(shards) > 0:
        drawn = steps_of(own_key, shape, shards, -0.22, 0.18) * drawn
    return jnp.clip(drawn, min=-reach, max=reach).astype(kind)


def setup_inputs(seed: int = 0) -> dict:
    key_list = jax.random.split(jax.random.key(seed), 6)
    return {
        "weights": bell_draw(key_list[0], (ROWS, COLS), 1.0, 6.0, ((0, 32), (1, 8)), jnp.float32),
        "factor_rows": bell_draw(key_list[1], (PIVOTS * BLOCK, COLS), (4 * BLOCK) ** -0.5, 0.25, ((0, 32), (1, 8))),
        "diag_inverse": draw_diag_inverse(jax.random.fold_in(key_list[5], 71), 0),
        "prune_tiles": place_ends((jax.random.randint(key_list[3], (ROWS // BLOCK, PIVOTS), 0, 2) < 1).astype(jnp.int32), jax.random.fold_in(key_list[3], 1), 0, 1),
        "pivot_order": draw_pivot_order(jax.random.fold_in(key_list[5], 71), 0),
    }


def reference(weights, factor_rows, diag_inverse, prune_tiles, pivot_order):
    nblocks = COLS // BLOCK
    current = weights
    finished = jnp.zeros((nblocks,), jnp.float32)
    block_ids = jnp.arange(nblocks, dtype=jnp.int32)
    pruned_all = jnp.repeat(prune_tiles.astype(jnp.float32), BLOCK, axis=0)
    for step in range(PIVOTS):
        block_id = pivot_order[step]
        start = (block_id * BLOCK).astype(jnp.int32)
        panel_now = lax.dynamic_slice_in_dim(current, start, BLOCK, 1)
        pruned = pruned_all[:, step:step + 1]
        errors = jnp.dot(panel_now, diag_inverse[step].astype(jnp.float32), precision=lax.Precision.HIGHEST) * pruned
        finished = jnp.maximum(finished, (block_ids == block_id).astype(jnp.float32))
        keep_cols = jnp.repeat(1.0 - finished, BLOCK)
        update = jnp.dot(errors, factor_rows[step * BLOCK:(step + 1) * BLOCK].astype(jnp.float32), precision=lax.Precision.HIGHEST)
        current = current - update * keep_cols[None, :]
        current = lax.dynamic_update_slice_in_dim(current, panel_now * (1.0 - pruned), start, 1)
    return current
```

```python
import jax
import jax.numpy as jnp
from jax import lax
from jax.experimental import pallas as pl
from jax.experimental.pallas import tpu as pltpu
from jax.sharding import PartitionSpec as P

BLOCK = 128
PIVOTS = 8
COLDEV = 8
ROWDEV = 32
Z = 8
CHUNK = 64
MESH = pl.DeviceIdType.MESH
ANY = pl.BlockSpec(memory_space=pl.ANY)
VM = pl.BlockSpec(memory_space=pltpu.VMEM)
SM = pl.BlockSpec(memory_space=pltpu.SMEM)


def prep_kernel(loc_ref, *refs):
    w_refs, f_refs = refs[:PIVOTS], refs[PIVOTS : 2 * PIVOTS]
    q_ref, s_ref, fp_ref = refs[2 * PIVOTS :]
    for k in range(PIVOTS):
        w = w_refs[k][...]
        top = jnp.maximum(jnp.max(jnp.abs(w), axis=0, keepdims=True), 1e-30)
        s_ref[0, k : k + 1, :] = top * (1.0 / 32767.0)
        q_ref[0, k] = jnp.round(w * (32767.0 / top)).astype(jnp.int32).astype(jnp.int16)

    @pl.when(pl.program_id(0) == 0)
    def _():
        for k in range(PIVOTS):
            fp_ref[k] = f_refs[k][...]


def prep(loc, weights, factor_rows):
    rows, frows = weights.shape[0], factor_rows.shape[0]
    chunks = rows // CHUNK

    def wspec(k):
        return pl.BlockSpec((CHUNK, BLOCK), lambda i, loc: (i, loc[k]))

    def fspec(k):
        return pl.BlockSpec((frows, BLOCK), lambda i, loc: (0, loc[k]))

    return pl.pallas_call(
        prep_kernel,
        grid_spec=pltpu.PrefetchScalarGridSpec(
            num_scalar_prefetch=1,
            grid=(chunks,),
            in_specs=[wspec(k) for k in range(PIVOTS)] + [fspec(k) for k in range(PIVOTS)],
            out_specs=[
                pl.BlockSpec((1, PIVOTS, CHUNK, BLOCK), lambda i, loc: (i, 0, 0, 0)),
                pl.BlockSpec((1, PIVOTS, BLOCK), lambda i, loc: (i, 0, 0)),
                pl.BlockSpec((PIVOTS, frows, BLOCK), lambda i, loc: (0, 0, 0)),
            ],
        ),
        out_shape=[
            jax.ShapeDtypeStruct((chunks, PIVOTS, CHUNK, BLOCK), jnp.int16),
            jax.ShapeDtypeStruct((chunks, PIVOTS, BLOCK), jnp.float32),
            jax.ShapeDtypeStruct((PIVOTS, frows, BLOCK), jnp.bfloat16),
        ],
        name="prep",
    )(loc, *[weights] * PIVOTS, *[factor_rows] * PIVOTS)


class Net:
    def __init__(self, send, recv, local):
        self.send, self.recv, self.local = send, recv, local
        self.sent, self.own_count = [], 0

    def remote(self, src, dst, device):
        i = len(self.sent)
        copy = pltpu.make_async_remote_copy(
            src_ref=src,
            dst_ref=dst,
            send_sem=self.send.at[i],
            recv_sem=self.recv.at[i],
            device_id=device,
            device_id_type=MESH,
        )
        copy.start()
        self.sent.append(copy)
        return copy

    def own(self, src, dst):
        copy = pltpu.make_async_copy(src, dst, self.local.at[self.own_count])
        self.own_count += 1
        copy.start()
        return copy

    def finish(self):
        for copy in self.sent:
            copy.wait_send()


class RowGather:
    def __init__(self, net, r, mine, out, half):
        core, xlo = lax.rem(r, 2), lax.rem(r // 2, 2)
        self.net, self.mine, self.out, self.half, self.r = net, mine, out, half, r
        self.sibling = r + 1 - 2 * core
        self.partner = r + 2 - 4 * xlo
        self.up, self.down = lax.rem(r + 4, ROWDEV), lax.rem(r + ROWDEV - 4, ROWDEV)
        self.flight, self.given = {}, []

    def origin(self, chain, step):
        base = self.r if chain == 0 else self.partner
        return lax.rem(base + 4 * step + ROWDEV, ROWDEV)

    def give(self, origin, src):
        self.given.append(self.net.remote(src, self.out.at[origin], {"row": self.sibling}))

    def launch(self, chain, step):
        a, b = self.origin(chain, -step), self.origin(chain, step)
        out, half = self.out, self.half
        if chain == 0 and step == 0:
            src_a = src_b = self.mine
        else:
            src_a, src_b = out.at[a], out.at[b]
        dst_a, dst_b = out.at[a], out.at[b]
        if step == 3:
            src_a, dst_a, src_b, dst_b = half(src_a, 0), half(dst_a, 0), half(src_b, 1), half(dst_b, 1)
        self.flight[chain] = (
            self.net.remote(src_a, dst_a, {"row": self.up}),
            self.net.remote(src_b, dst_b, {"row": self.down}),
        )

    def begin(self):
        self.first = self.net.remote(self.mine, self.out.at[self.r], {"row": self.partner})
        self.launch(0, 0)
        self.give(self.r, self.mine)

    def stage(self, i):
        if i == 0:
            self.first.wait_recv()
            self.launch(1, 0)
            self.give(self.partner, self.out.at[self.partner])
            return
        chain, step = (i - 1) % 2, (i - 1) // 2
        for copy in self.flight[chain]:
            copy.wait_recv()
        if step < 3:
            self.launch(chain, step + 1)
            for o in (self.origin(chain, -step - 1), self.origin(chain, step + 1)):
                self.give(o, self.out.at[o])
        else:
            o = self.origin(chain, 4)
            self.give(o, self.out.at[o])

    def finish(self):
        for copy in self.given:
            copy.wait_recv()


STAGES = 9


def comm_kernel(piv, q, s, fp, f, qo, so, fo, po, rq, rs, r1, selq, sels, sel1, send, recv, local):
    me = lax.axis_index("col")
    r = lax.axis_index("row")
    blocks_dev = f.shape[1] // BLOCK
    cols = [lax.rem(me + d, COLDEV) for d in range(1, COLDEV)]
    net = Net(send, recv, local)
    fg = RowGather(net, r, f, fo, lambda ref, h: ref.at[pl.ds(16 * h, 16), :])
    pg = RowGather(net, r, po.at[r], po, lambda ref, h: ref.at[pl.ds(4 * h, 4)])

    barrier = pltpu.get_barrier_semaphore()
    for c in cols:
        pl.semaphore_signal(barrier, inc=1, device_id={"col": c}, device_id_type=MESH)
    for n in (fg.sibling, fg.partner, fg.up, fg.down):
        pl.semaphore_signal(barrier, inc=1, device_id={"row": n}, device_id_type=MESH)
    pl.semaphore_wait(barrier, COLDEV - 1 + 4)

    def to_cols(src_of, dst):
        return [net.remote(src_of(c), dst, {"col": c}) for c in cols]

    fp1 = to_cols(lambda c: fp.at[c], r1.at[me])
    fp1_own = net.own(fp.at[me], r1.at[me])
    fg.begin()
    f_own = net.own(f, fo.at[r])

    fp1_own.wait()
    for copy in fp1:
        copy.wait_recv()
    sel1[...] = r1[piv[me] // blocks_dev]
    fp2 = to_cols(lambda c: sel1, po.at[r, me])
    fp2_own = net.own(sel1, po.at[r, me])

    w1 = to_cols(lambda c: q.at[c], rq.at[me]) + to_cols(lambda c: s.at[c], rs.at[me])
    w1_own = [net.own(q.at[me], rq.at[me]), net.own(s.at[me], rs.at[me])]

    fp2_own.wait()
    for copy in fp2:
        copy.wait_recv()
    pg.begin()
    fg.stage(0)
    pg.stage(0)
    for i in range(1, 5):
        pg.stage(i)
        fg.stage(i)

    for copy in w1_own:
        copy.wait()
    for copy in w1:
        copy.wait_recv()
    for k in range(PIVOTS):
        owner = piv[k] // blocks_dev
        selq[k] = rq[owner, k]
        sels[k : k + 1, :] = rs[owner, k : k + 1, :]
    w2 = to_cols(lambda c: selq, qo.at[me]) + to_cols(lambda c: sels, so.at[me])
    w2_own = [net.own(selq, qo.at[me]), net.own(sels, so.at[me])]

    for i in range(5, STAGES):
        pg.stage(i)
        fg.stage(i)
    for copy in w2_own:
        copy.wait()
    for copy in w2:
        copy.wait_recv()
    pg.finish()
    fg.finish()
    f_own.wait()
    net.finish()


def comm(pivot_order, q, s, fp, f):
    frows, width = f.shape
    copies = 6 * (COLDEV - 1) + 2 * (1 + 16 + 16)
    return pl.pallas_call(
        comm_kernel,
        in_specs=[SM, ANY, ANY, ANY, ANY],
        out_specs=[ANY] * 4,
        out_shape=[
            jax.ShapeDtypeStruct(q.shape, q.dtype),
            jax.ShapeDtypeStruct(s.shape, s.dtype),
            jax.ShapeDtypeStruct((ROWDEV, frows, width), f.dtype),
            jax.ShapeDtypeStruct((ROWDEV,) + fp.shape, fp.dtype),
        ],
        scratch_shapes=[
            pltpu.VMEM(q.shape, q.dtype),
            pltpu.VMEM(s.shape, s.dtype),
            pltpu.VMEM(fp.shape, fp.dtype),
            pltpu.VMEM(q.shape[1:], q.dtype),
            pltpu.VMEM(s.shape[1:], s.dtype),
            pltpu.VMEM(fp.shape[1:], fp.dtype),
            pltpu.SemaphoreType.DMA((copies,)),
            pltpu.SemaphoreType.DMA((copies,)),
            pltpu.SemaphoreType.DMA((8,)),
        ],
        compiler_params=pltpu.CompilerParams(collective_id=0, has_side_effects=True),
        name="comm",
    )(pivot_order, q, s, fp, f)


def split(x):
    hi = x.astype(jnp.bfloat16)
    return hi, (x - hi.astype(jnp.float32)).astype(jnp.bfloat16)


def dot(a, b):
    return jnp.dot(a, b, preferred_element_type=jnp.float32)


def update_kernel(steps, prune, w, f, q, s, fp, d, out, ehi, elo, pan):
    rows, width = w.shape
    tile = pl.program_id(0)

    def by_tile(values):
        at = lax.broadcasted_iota(jnp.int32, (rows, 1), 0) // BLOCK
        column = jnp.full((rows, 1), values[0], jnp.float32)
        for t in range(1, len(values)):
            column = jnp.where(at == t, values[t], column)
        return column

    @pl.when(tile == 0)
    def _():
        for k in range(PIVOTS):
            coded = q[:, k].astype(jnp.int32).astype(jnp.float32)
            panel = (coded * s[:, k : k + 1, :]).reshape(rows, BLOCK)
            if k > 0:
                depth = k * BLOCK
                factor = fp[: 4 * k, k].reshape(depth, BLOCK)
                panel = panel - (dot(ehi[:, :depth], factor) + dot(elo[:, :depth], factor))
            hi, lo = split(panel)
            errors = dot(hi, d[k]) + dot(lo, d[k])
            errors = errors * by_tile([prune[t, k].astype(jnp.float32) for t in range(rows // BLOCK)])
            hi, lo = split(errors)
            ehi[:, k * BLOCK : (k + 1) * BLOCK] = hi
            elo[:, k * BLOCK : (k + 1) * BLOCK] = lo

    depth = lax.broadcasted_iota(jnp.int32, (f.shape[0], BLOCK), 0) // BLOCK
    blocks = width // BLOCK
    parts = []
    for b in range(blocks):
        part = f[:, b * BLOCK : (b + 1) * BLOCK]
        parts.append(jnp.where(depth < steps[tile * blocks + b], part, jnp.zeros_like(part)))
    masked = jnp.concatenate(parts, axis=1)
    new = w[...] - (dot(ehi[...], masked) + dot(elo[...], masked))
    for b in range(blocks):
        step = steps[tile * blocks + b]
        for t in range(rows // BLOCK):
            pruned = prune[t, jnp.minimum(step, PIVOTS - 1)].astype(jnp.float32)
            keep = jnp.where(step < PIVOTS, 1.0 - pruned, 1.0)
            out[t * BLOCK : (t + 1) * BLOCK, b * BLOCK : (b + 1) * BLOCK] = (
                new[t * BLOCK : (t + 1) * BLOCK, b * BLOCK : (b + 1) * BLOCK] * keep
            )


def update(steps, prune, w, f, q, s, fp, d):
    rows, width = w.shape
    tile = 256
    whole = lambda a: pl.BlockSpec(a.shape, lambda i, *_: (0,) * a.ndim)
    return pl.pallas_call(
        update_kernel,
        grid_spec=pltpu.PrefetchScalarGridSpec(
            num_scalar_prefetch=2,
            grid=(width // tile,),
            in_specs=[
                pl.BlockSpec((rows, tile), lambda i, *_: (0, i)),
                pl.BlockSpec((f.shape[0], tile), lambda i, *_: (0, i)),
                whole(q),
                whole(s),
                whole(fp),
                whole(d),
            ],
            out_specs=pl.BlockSpec((rows, tile), lambda i, *_: (0, i)),
            scratch_shapes=[
                pltpu.VMEM((rows, f.shape[0]), jnp.bfloat16),
                pltpu.VMEM((rows, f.shape[0]), jnp.bfloat16),
                pltpu.VMEM((rows, BLOCK), jnp.float32),
            ],
        ),
        out_shape=jax.ShapeDtypeStruct(w.shape, w.dtype),
        compiler_params=pltpu.CompilerParams(vmem_limit_bytes=48 * 2**20),
        name="update",
    )(steps, prune, w, f, q, s, fp, d)


def shards(weights, factor_rows, diag_inverse, prune_tiles, pivot_order):
    blocks_dev = weights.shape[1] // BLOCK
    q, s, fp = prep(pivot_order % blocks_dev, weights, factor_rows)
    q, s, f, fp = comm(pivot_order, q, s, fp, factor_rows)
    f = f.reshape(-1, f.shape[-1])
    ids = lax.axis_index("col") * blocks_dev + jnp.arange(blocks_dev, dtype=jnp.int32)
    hit = ids[:, None] == pivot_order[None, :]
    steps = jnp.min(jnp.where(hit, jnp.arange(PIVOTS, dtype=jnp.int32)[None], PIVOTS), axis=1)
    return update(steps, prune_tiles, weights, f, q, s, fp, diag_inverse)


def solution(mesh):
    return jax.shard_map(
        shards,
        mesh=mesh,
        in_specs=(P("row", "col"), P("row", "col"), P(), P("row", None), P()),
        out_specs=P("row", "col"),
        check_vma=False,
    )
```

```python
import functools

import jax
import jax.numpy as jnp
from jax import lax
from jax.experimental import pallas as pl
from jax.experimental.pallas import tpu as pltpu
from jax.sharding import PartitionSpec as P

BLOCK = 128
PIVOTS = 8
COLDEV = 8
ROWDEV = 32
Z = 8
CHUNK = 64
VMEM = 62 * 2**20
MESH = pl.DeviceIdType.MESH
ANY = pl.BlockSpec(memory_space=pl.ANY)
VM = pl.BlockSpec(memory_space=pltpu.VMEM)
SM = pl.BlockSpec(memory_space=pltpu.SMEM)


def once(copy):
    return [(None, copy)]


def each(cases, act):
    for when, copy in cases:
        if when is None:
            act(copy)
        else:
            pl.when(when)(lambda copy=copy: act(copy))


class Net:
    def __init__(self, send, recv, local):
        self.send, self.recv, self.local = send, recv, local
        self.sent, self.own_count = [], 0

    def make(self, i, src, dst, device, land=None):
        return pltpu.make_async_remote_copy(
            src_ref=src,
            dst_ref=dst,
            send_sem=self.send.at[i],
            recv_sem=self.recv.at[i if land is None else land],
            device_id=device,
            device_id_type=MESH,
        )

    def remote(self, src, dst, device):
        copy = self.make(len(self.sent), src, dst, device)
        copy.start()
        self.sent.append(once(copy))
        return copy

    def shard(self, out, origin, cut, device, arriving, src=None):
        i = len(self.sent)

        def cases(o, src):
            made = []
            for when, view in cut(o):
                made.append((when, self.make(i, view(out.at[o] if src is None else src), view(out.at[o]), device)))
            return made

        sends = cases(origin, src)
        each(sends, lambda copy: copy.start())
        self.sent.append(sends)
        lands = cases(arriving, None)
        return lambda: each(lands, lambda copy: copy.wait_recv())

    def some(self, sends, lands, land=None):
        i = len(self.sent)
        cases = [(when, self.make(i, src, dst, device, land)) for when, src, dst, device in sends]
        each(cases, lambda copy: copy.start())
        self.sent.append(cases)
        return lambda: self.take(lands, i)

    def take(self, lands, i):
        cases = [(when, self.make(i, ref, ref, {"row": lax.axis_index("row")})) for when, ref in lands]
        each(cases, lambda copy: copy.wait_recv())

    def own(self, src, dst):
        copy = pltpu.make_async_copy(src, dst, self.local.at[self.own_count])
        self.own_count += 1
        copy.start()
        return copy

    def blocks(self, src, dst):
        sem = self.local.at[self.own_count]
        self.own_count += 1
        for b in range(dst.shape[0]):
            pltpu.make_async_copy(src.at[:, pl.ds(b * BLOCK, BLOCK)], dst.at[b], sem).start()
        return pltpu.make_async_copy(dst, dst, sem)

    def finish(self):
        for cases in self.sent:
            each(cases, lambda copy: copy.wait_send())


class Row:
    def __init__(self):
        r = lax.axis_index("row")
        core, xlo = lax.rem(r, 2), lax.rem(r // 2, 2)
        self.me, self.core, self.z = r, core, r // 4
        self.group = 2 * core + xlo
        self.sibling = r + 1 - 2 * core
        self.partner = r + 2 - 4 * xlo
        self.across = self.sibling + self.partner - r
        self.up, self.down = self.along(r, 1), self.along(r, -1)

    def along(self, base, steps):
        return lax.rem(base + 4 * steps + ROWDEV, ROWDEV)


def row_gather(net, row, out, cut, half, mine=None):
    given = []

    def give(origin, arriving, src=None):
        given.append(net.shard(out, origin, cut, {"row": row.sibling}, arriving, src))

    def launch(base, step, src=None):
        up, down = row.along(base, -step), row.along(base, step)
        part = [cut, cut] if step < 3 else [half(0), half(1)]
        return [
            net.shard(out, up, part[0], {"row": row.up}, row.along(base, -step - 1), src),
            net.shard(out, down, part[1], {"row": row.down}, row.along(base, step + 1), src),
        ]

    first = net.shard(out, row.me, cut, {"row": row.partner}, row.partner, mine)
    flight = [launch(row.me, 0, mine), None]
    give(row.me, row.sibling, mine)
    yield
    first()
    flight[1] = launch(row.partner, 0)
    give(row.partner, row.across)
    yield
    for step in range(4):
        for chain, base, other in ((0, row.me, row.sibling), (1, row.partner, row.across)):
            for landed in flight[chain]:
                landed()
            if step < 3:
                flight[chain] = launch(base, step + 1)
                give(row.along(base, -step - 1), row.along(other, -step - 1))
                give(row.along(base, step + 1), row.along(other, step + 1))
            else:
                give(row.along(base, 4), row.along(other, 4))
            yield
    for landed in given:
        landed()
    yield


def whole(origin):
    return [(None, lambda ref: ref)]


def rows_half(h):
    return lambda origin: [(None, lambda ref: ref.at[pl.ds(16 * h, 16), :])]


def split(x):
    hi = x.astype(jnp.bfloat16)
    return hi, (x - hi.astype(jnp.float32)).astype(jnp.bfloat16)


def dot(a, b):
    return jnp.dot(a, b, preferred_element_type=jnp.float32)


COPIES = 108
ORDER = "PFWPFFPFWFPWWPFPFWWRFRRFRRFRRR"


def comm_kernel(
    slots, piv, prune, w, f, d, fo, eo_hi, eo_lo,
    wv, fv, dv, fpv, r1, sel1, pv, q, s, rq, rs, selq, sels, qv, sv, ehi, elo, send, recv, local,
):
    me = lax.axis_index("col")
    row = Row()
    rows = w.shape[0]
    blocks_dev = f.shape[1] // BLOCK
    cols = [lax.rem(me + d, COLDEV) for d in (2, 6, 1, 7, 4, 3, 5)]
    planes = [1, -1, 2, -2, 3, -3, 4]
    net = Net(send, recv, local)

    load_f, load_w, load_d = net.blocks(f, fv), net.blocks(w, wv), net.own(d, dv)
    barrier = pltpu.get_barrier_semaphore()
    for c in cols:
        pl.semaphore_signal(barrier, inc=1, device_id={"col": c}, device_id_type=MESH)
    for n in [row.sibling, row.partner] + [row.along(row.me, p) for p in planes]:
        pl.semaphore_signal(barrier, inc=1, device_id={"row": n}, device_id_type=MESH)

    def to_cols(src_of, dst, peers=cols):
        return [net.remote(src_of(c), dst, {"col": c}) for c in peers]

    base = COPIES - PIVOTS

    def owners_of(k):
        return piv[k] // blocks_dev

    def place(k):
        return lax.rem(piv[k], blocks_dev)

    def factor():
        keep = net.own(f, fo.at[row.me])
        yield from row_gather(net, row, fo, whole, rows_half, f)
        keep.wait()
        yield

    def pivot_columns():
        load_f.wait()
        for k in range(1, PIVOTS):
            fpv[k] = fv[place(k)]
        pl.semaphore_wait(barrier, COLDEV - 1 + 9)
        hop = [net.some([(c > row.z, fpv.at[c], r1.at[me], {"col": c})], [(me > row.z, r1.at[me])]) for c in cols]
        yield
        for landed in hop:
            landed()

        @pl.when(me > row.z)
        def _():
            r1[me] = fpv[me]
            sel1[...] = r1[owners_of(me)]
            pv[me, row.group, row.z] = sel1[...]

        hop = []
        for p in planes:
            origin = row.along(row.me, -p) // 4
            hop.append(
                net.some(
                    [(me > row.z, sel1, pv.at[me, row.group, row.z], {"row": row.along(row.me, p)})],
                    [(me > origin, sel1)],
                )
            )
        yield
        for landed in hop:
            landed()
        for c in cols:
            sends = []
            for k in range(1, PIVOTS):
                above = pv.at[k, row.group, pl.ds(0, k)]
                sends.append((me == k, above, above, {"col": c}))
            net.some(sends, [], base + me)
        yield
        hop = []
        for k in range(1, PIVOTS):
            above = pv.at[k, row.group, pl.ds(0, k)]
            net.take([(me != k, above)], base + k)
            hop.append(net.some([(None, above, above, {"row": row.partner})], [(None, above)]))
        yield
        last = []
        for k, landed in zip(range(1, PIVOTS), hop):
            landed()
            above = pv.at[k, pl.ds(2 * row.core, 2), pl.ds(0, k)]
            last.append(net.some([(None, above, above, {"row": row.sibling})], [(None, above)]))
        yield
        for landed in last:
            landed()
        yield

    owners = [piv[k] // blocks_dev for k in range(PIVOTS)]
    ranks = [sum(((owners[i] == owners[k]).astype(jnp.int32) for i in range(k)), jnp.int32(0)) for k in range(PIVOTS)]

    def place_of_slot(i):
        start = jnp.int32(0)
        for k in range(PIVOTS):
            start = jnp.where((owners[k] == me) & (ranks[k] == i), place(k), start)
        return start

    def encode(chunk, qdst, sdst):
        rows_c = pl.ds(pl.multiple_of(chunk * CHUNK, CHUNK), CHUNK)
        for i in range(slots):
            block = wv[starts[i], rows_c]
            top = jnp.maximum(jnp.max(jnp.abs(block), axis=0, keepdims=True), 1e-30)
            sdst[i : i + 1, :] = top * (1.0 / 32767.0)
            qdst[i] = jnp.round(block * (32767.0 / top)).astype(jnp.int32).astype(jnp.int16)

    starts = [place_of_slot(i) for i in range(slots)]

    def panels():
        load_w.wait()
        hop = []
        for c in cols:
            encode(c, q.at[c], s.at[c])
            hop += to_cols(lambda c: s.at[c], rs.at[me], [c]) + to_cols(lambda c: q.at[c], rq.at[me], [c])
        encode(me, rq.at[me], rs.at[me])
        yield
        for copy in hop:
            copy.wait_recv()
        at_slot = lax.broadcasted_iota(jnp.int32, sels.shape, 0)
        for k in range(PIVOTS):
            slot = jnp.minimum(ranks[k], slots - 1)
            selq[k] = rq[owners[k], slot]
            picked = jnp.where(at_slot == slot, rs[owners[k]], 0.0)
            sels[k : k + 1, :] = jnp.sum(picked, axis=0, keepdims=True)
        beside = me + 1 - 2 * lax.rem(me, 2)
        ahead, behind = lax.rem(me + 2, COLDEV), lax.rem(me + 6, COLDEV)
        beside_ahead, beside_behind = lax.rem(beside + 2, COLDEV), lax.rem(beside + 6, COLDEV)
        across = net.remote(selq, qv.at[me], {"col": beside})
        first = [net.remote(selq, qv.at[me], {"col": c}) for c in (ahead, behind)]
        scales = to_cols(lambda c: sels, sv.at[me])
        keep = [net.own(selq, qv.at[me]), net.own(sels, sv.at[me])]
        yield
        across.wait_recv()
        second = [net.remote(qv.at[beside], qv.at[beside], {"col": c}) for c in (ahead, behind)]
        yield

        def pass_on(landed, from_behind, from_ahead):
            for copy in landed:
                copy.wait_recv()
            low, high = qv.at[from_behind, pl.ds(0, 4)], qv.at[from_ahead, pl.ds(4, 4)]
            return [net.remote(low, low, {"col": ahead}), net.remote(high, high, {"col": behind})]

        last = pass_on(first, behind, ahead)
        yield
        last += pass_on(second, beside_behind, beside_ahead)
        yield
        for copy in keep:
            copy.wait()
        for copy in last + scales:
            copy.wait_recv()
        yield

    def by_tile(values):
        at = lax.broadcasted_iota(jnp.int32, (rows, 1), 0) // BLOCK
        column = jnp.full((rows, 1), values[0], jnp.float32)
        for t in range(1, len(values)):
            column = jnp.where(at == t, values[t], column)
        return column

    def eliminate():
        load_d.wait()
        stores = []
        for k in range(PIVOTS):
            coded = qv[:, k].astype(jnp.int32).astype(jnp.float32)
            panel = (coded * sv[:, k : k + 1, :]).reshape(rows, BLOCK)
            if k > 0:
                depth = k * BLOCK
                block = jnp.concatenate([pv[k, g, j] for j in range(k) for g in (0, 2, 1, 3)], axis=0)
                panel = panel - (dot(ehi[:, :depth], block) + dot(elo[:, :depth], block))
            hi, lo = split(panel)
            errors = dot(hi, dv[k]) + dot(lo, dv[k])
            errors = errors * by_tile([prune[t, k].astype(jnp.float32) for t in range(rows // BLOCK)])
            hi, lo = split(errors)
            ehi[:, k * BLOCK : (k + 1) * BLOCK] = hi
            elo[:, k * BLOCK : (k + 1) * BLOCK] = lo
            yield
        stores = [net.own(ehi, eo_hi), net.own(elo, eo_lo)]
        yield
        for copy in stores:
            copy.wait()
        yield

    streams = {"P": pivot_columns, "F": factor, "W": panels, "R": eliminate}
    streams = {name: stream() for name, stream in streams.items()}
    for name in ORDER:
        next(streams[name], None)
    for stream in streams.values():
        for _ in stream:
            pass
    net.finish()


def comm(slots, pivot_order, prune, w, f, d):
    (rows, width), frows = w.shape, f.shape[0]
    chunks, depth = rows // CHUNK, PIVOTS * BLOCK
    q = pltpu.VMEM((chunks, PIVOTS, CHUNK, BLOCK), jnp.int16)
    s = pltpu.VMEM((chunks, PIVOTS, BLOCK), jnp.float32)
    sent_q = pltpu.VMEM((COLDEV, slots, CHUNK, BLOCK), jnp.int16)
    sent_s = pltpu.VMEM((COLDEV, PIVOTS, BLOCK), jnp.float32)
    columns = pltpu.VMEM((PIVOTS, frows, BLOCK), f.dtype)
    errors = pltpu.VMEM((rows, depth), jnp.bfloat16)
    return pl.pallas_call(
        functools.partial(comm_kernel, slots),
        in_specs=[SM, SM, ANY, ANY, ANY],
        out_specs=[ANY] * 3,
        out_shape=[
            jax.ShapeDtypeStruct((ROWDEV, frows, width), f.dtype),
            jax.ShapeDtypeStruct((rows, depth), jnp.bfloat16),
            jax.ShapeDtypeStruct((rows, depth), jnp.bfloat16),
        ],
        scratch_shapes=[
            pltpu.VMEM((width // BLOCK, rows, BLOCK), w.dtype),
            pltpu.VMEM((width // BLOCK, frows, BLOCK), f.dtype),
            pltpu.VMEM(d.shape, d.dtype),
            columns,
            columns,
            pltpu.VMEM((frows, BLOCK), f.dtype),
            pltpu.VMEM((PIVOTS, 4, Z, frows, BLOCK), f.dtype),
            sent_q,
            sent_s,
            sent_q,
            sent_s,
            pltpu.VMEM((PIVOTS, CHUNK, BLOCK), jnp.int16),
            pltpu.VMEM((PIVOTS, BLOCK), jnp.float32),
            q,
            s,
            errors,
            errors,
            pltpu.SemaphoreType.DMA((COPIES,)),
            pltpu.SemaphoreType.DMA((COPIES,)),
            pltpu.SemaphoreType.DMA((16,)),
        ],
        compiler_params=pltpu.CompilerParams(collective_id=0 if slots < PIVOTS else 1, has_side_effects=True, vmem_limit_bytes=VMEM),
        name="comm",
    )(pivot_order, prune, w, f, d)


def update_kernel(piv, prune, w, f, ehi, elo, out):
    rows, width = w.shape
    blocks = width // BLOCK
    total = pl.num_programs(0) * blocks
    first = lax.axis_index("col") * total + pl.program_id(0) * blocks
    steps = []
    for b in range(blocks):
        step = jnp.int32(PIVOTS)
        for k in range(PIVOTS):
            step = jnp.where(piv[k] == first + b, k, step)
        steps.append(step)

        @pl.loop(step, PIVOTS)
        def _(j, b=b):
            rows_j = pl.ds(pl.multiple_of(j * BLOCK, BLOCK), BLOCK)
            f[rows_j, b * BLOCK : (b + 1) * BLOCK] = jnp.zeros((BLOCK, BLOCK), f.dtype)

    new = w[...] - (dot(ehi[...], f[...]) + dot(elo[...], f[...]))
    for b, step in enumerate(steps):
        for t in range(rows // BLOCK):
            pruned = prune[t, jnp.minimum(step, PIVOTS - 1)].astype(jnp.float32)
            keep = jnp.where(step < PIVOTS, 1.0 - pruned, 1.0)
            here = slice(t * BLOCK, (t + 1) * BLOCK), slice(b * BLOCK, (b + 1) * BLOCK)
            out[here] = new[here] * keep


TILE = 512


def update(pivot_order, prune, w, f, ehi, elo):
    rows, width = w.shape
    resident = pl.BlockSpec(ehi.shape, lambda i, *_: (0, 0), pipeline_mode=pl.Buffered(1))
    return pl.pallas_call(
        update_kernel,
        grid_spec=pltpu.PrefetchScalarGridSpec(
            num_scalar_prefetch=2,
            grid=(width // TILE,),
            in_specs=[
                pl.BlockSpec((rows, TILE), lambda i, *_: (0, i)),
                pl.BlockSpec((f.shape[0], TILE), lambda i, *_: (0, i)),
                resident,
                resident,
            ],
            out_specs=pl.BlockSpec((rows, TILE), lambda i, *_: (0, i)),
        ),
        out_shape=jax.ShapeDtypeStruct(w.shape, w.dtype),
        compiler_params=pltpu.CompilerParams(vmem_limit_bytes=VMEM),
        name="update",
    )(pivot_order, prune, w, f, ehi, elo)


SLOTS = 4


def shards(weights, factor_rows, diag_inverse, prune_tiles, pivot_order):
    owners = pivot_order // (weights.shape[1] // BLOCK)
    most = jnp.max(jnp.sum((owners[:, None] == owners[None, :]).astype(jnp.int32), axis=1))
    f, ehi, elo = lax.cond(
        most <= SLOTS,
        functools.partial(comm, SLOTS),
        functools.partial(comm, PIVOTS),
        pivot_order,
        prune_tiles,
        weights,
        factor_rows,
        diag_inverse,
    )
    return update(pivot_order, prune_tiles, weights, f.reshape(-1, f.shape[-1]), ehi, elo)


def solution(mesh):
    return jax.shard_map(
        shards,
        mesh=mesh,
        in_specs=(P("row", "col"), P("row", "col"), P(), P("row", None), P()),
        out_specs=P("row", "col"),
        check_vma=False,
    )
```

```python
import functools

import jax
import jax.numpy as jnp
from jax import lax
from jax.experimental import pallas as pl
from jax.experimental.pallas import tpu as pltpu
from jax.sharding import PartitionSpec as P

BLOCK = 128
PIVOTS = 8
COLDEV = 8
ROWDEV = 32
Z = 8
CHUNK = 64
VMEM = 58 * 2**20
MESH = pl.DeviceIdType.MESH
ANY = pl.BlockSpec(memory_space=pl.ANY)
VM = pl.BlockSpec(memory_space=pltpu.VMEM)
SM = pl.BlockSpec(memory_space=pltpu.SMEM)


def once(copy):
    return [(None, copy)]


def each(cases, act):
    for when, copy in cases:
        if when is None:
            act(copy)
        else:
            pl.when(when)(lambda copy=copy: act(copy))


class Net:
    def __init__(self, send, recv, local):
        self.send, self.recv, self.local = send, recv, local
        self.sent, self.own_count = [], 0

    def make(self, i, src, dst, device, land=None):
        return pltpu.make_async_remote_copy(
            src_ref=src,
            dst_ref=dst,
            send_sem=self.send.at[i],
            recv_sem=self.recv.at[i if land is None else land],
            device_id=device,
            device_id_type=MESH,
        )

    def remote(self, src, dst, device):
        copy = self.make(len(self.sent), src, dst, device)
        copy.start()
        self.sent.append(once(copy))
        return copy

    def shard(self, out, origin, cut, device, arriving, src=None):
        i = len(self.sent)

        def cases(o, src):
            made = []
            for when, view in cut(o):
                made.append((when, self.make(i, view(out.at[o] if src is None else src), view(out.at[o]), device)))
            return made

        sends = cases(origin, src)
        each(sends, lambda copy: copy.start())
        self.sent.append(sends)
        lands = cases(arriving, None)
        return lambda: each(lands, lambda copy: copy.wait_recv())

    def some(self, sends, lands, land=None):
        i = len(self.sent)
        cases = [(when, self.make(i, src, dst, device, land)) for when, src, dst, device in sends]
        each(cases, lambda copy: copy.start())
        self.sent.append(cases)
        return lambda: self.take(lands, i)

    def take(self, lands, i):
        cases = [(when, self.make(i, ref, ref, {"row": lax.axis_index("row")})) for when, ref in lands]
        each(cases, lambda copy: copy.wait_recv())

    def own(self, src, dst):
        copy = pltpu.make_async_copy(src, dst, self.local.at[self.own_count])
        self.own_count += 1
        copy.start()
        return copy

    def blocks(self, src, dst):
        sem = self.local.at[self.own_count]
        self.own_count += 1
        for b in range(dst.shape[0]):
            pltpu.make_async_copy(src.at[:, pl.ds(b * BLOCK, BLOCK)], dst.at[b], sem).start()
        return pltpu.make_async_copy(dst, dst, sem)

    def finish(self):
        for cases in self.sent:
            each(cases, lambda copy: copy.wait_send())


class Row:
    def __init__(self):
        r = lax.axis_index("row")
        core, xlo = lax.rem(r, 2), lax.rem(r // 2, 2)
        self.me, self.core, self.z = r, core, r // 4
        self.group = 2 * core + xlo
        self.sibling = r + 1 - 2 * core
        self.partner = r + 2 - 4 * xlo
        self.across = self.sibling + self.partner - r
        self.up, self.down = self.along(r, 1), self.along(r, -1)

    def along(self, base, steps):
        return lax.rem(base + 4 * steps + ROWDEV, ROWDEV)


def row_gather(net, row, out, cut, half, mine, given):
    def give(distance, origin, arriving, src=None):
        landed = net.shard(out, origin, cut, {"row": row.sibling}, arriving, src)
        given.setdefault(distance, []).append(landed)

    def launch(base, step, src=None):
        up, down = row.along(base, -step), row.along(base, step)
        part = [cut, cut] if step < 3 else [half(0), half(1)]
        return [
            net.shard(out, up, part[0], {"row": row.up}, row.along(base, -step - 1), src),
            net.shard(out, down, part[1], {"row": row.down}, row.along(base, step + 1), src),
        ]

    first = net.shard(out, row.me, cut, {"row": row.partner}, row.partner, mine)
    flight = [launch(row.me, 0, mine), None]
    give(0, row.me, row.sibling, mine)
    yield
    first()
    flight[1] = launch(row.partner, 0)
    give(0, row.partner, row.across)
    yield
    for step in range(4):
        for chain, base, other in ((0, row.me, row.sibling), (1, row.partner, row.across)):
            for landed in flight[chain]:
                landed()
            if step < 3:
                flight[chain] = launch(base, step + 1)
                give(step + 1, row.along(base, -step - 1), row.along(other, -step - 1))
                give(step + 1, row.along(base, step + 1), row.along(other, step + 1))
            else:
                give(4, row.along(base, 4), row.along(other, 4))
            yield


def whole(origin):
    return [(None, lambda ref: ref)]


def rows_half(h):
    return lambda origin: [(None, lambda ref: ref.at[pl.ds(16 * h, 16), :])]


def split(x):
    hi = x.astype(jnp.bfloat16)
    return hi, (x - hi.astype(jnp.float32)).astype(jnp.bfloat16)


def dot(a, b):
    return jnp.dot(a, b, preferred_element_type=jnp.float32)


COPIES = 108
ORDER = "PFWPFPFWFPWFWPFPWFWFRRRRFRRRRFUFFFUU"
BATCHES = ((0, -1, 1, -2, 2), (-3, 3, 4))
SPAN = 1024


def comm_kernel(
    slots, piv, prune, w, f, d, out,
    wv, fv, dv, fpv, r1, sel1, pv, q, s, rq, rs, selq, sels, qv, sv, ev, fo, send, recv, local,
):
    me = lax.axis_index("col")
    row = Row()
    rows = w.shape[0]
    blocks_dev = f.shape[1] // BLOCK
    cols = [lax.rem(me + d, COLDEV) for d in (2, 6, 1, 7, 4, 3, 5)]
    planes = [1, -1, 2, -2, 3, -3, 4]
    net = Net(send, recv, local)

    load_f, load_w, load_d = net.blocks(f, fv), net.blocks(w, wv), net.own(d, dv)
    barrier = pltpu.get_barrier_semaphore()
    for c in cols:
        pl.semaphore_signal(barrier, inc=1, device_id={"col": c}, device_id_type=MESH)
    for n in [row.sibling, row.partner] + [row.along(row.me, p) for p in planes]:
        pl.semaphore_signal(barrier, inc=1, device_id={"row": n}, device_id_type=MESH)

    def to_cols(src_of, dst, peers=cols):
        return [net.remote(src_of(c), dst, {"col": c}) for c in peers]

    base = COPIES - PIVOTS

    def owners_of(k):
        return piv[k] // blocks_dev

    def place(k):
        return lax.rem(piv[k], blocks_dev)

    given = {}

    def factor():
        keep = net.own(f, fo.at[row.me])
        gather = row_gather(net, row, fo, whole, rows_half, f, given)
        next(gather)
        yield
        keep.wait()
        yield from gather

    def pivot_columns():
        load_f.wait()
        for k in range(1, PIVOTS):
            fpv[k] = fv[place(k)]
        pl.semaphore_wait(barrier, COLDEV - 1 + 9)
        hop = [net.some([(c > row.z, fpv.at[c], r1.at[me], {"col": c})], [(me > row.z, r1.at[me])]) for c in cols]
        yield
        for landed in hop:
            landed()

        @pl.when(me > row.z)
        def _():
            r1[me] = fpv[me]
            sel1[...] = r1[owners_of(me)]
            pv[me, row.group, row.z] = sel1[...]

        hop = []
        for p in planes:
            origin = row.along(row.me, -p) // 4
            hop.append(
                net.some(
                    [(me > row.z, sel1, pv.at[me, row.group, row.z], {"row": row.along(row.me, p)})],
                    [(me > origin, sel1)],
                )
            )
        yield
        for landed in hop:
            landed()
        for c in cols:
            sends = []
            for k in range(1, PIVOTS):
                above = pv.at[k, row.group, pl.ds(0, k)]
                sends.append((me == k, above, above, {"col": c}))
            net.some(sends, [], base + me)
        yield
        hop = []
        for k in range(1, PIVOTS):
            above = pv.at[k, row.group, pl.ds(0, k)]
            net.take([(me != k, above)], base + k)
            hop.append(net.some([(None, above, above, {"row": row.partner})], [(None, above)]))
        yield
        last = []
        for k, landed in zip(range(1, PIVOTS), hop):
            landed()
            above = pv.at[k, pl.ds(2 * row.core, 2), pl.ds(0, k)]
            last.append(net.some([(None, above, above, {"row": row.sibling})], [(None, above)]))
        yield
        for landed in last:
            landed()
        yield

    owners = [piv[k] // blocks_dev for k in range(PIVOTS)]
    ranks = [sum(((owners[i] == owners[k]).astype(jnp.int32) for i in range(k)), jnp.int32(0)) for k in range(PIVOTS)]

    def place_of_slot(i):
        start = jnp.int32(0)
        for k in range(PIVOTS):
            start = jnp.where((owners[k] == me) & (ranks[k] == i), place(k), start)
        return start

    def encode(chunk, qdst, sdst):
        rows_c = pl.ds(pl.multiple_of(chunk * CHUNK, CHUNK), CHUNK)
        for i in range(slots):
            block = wv[starts[i], rows_c]
            top = jnp.maximum(jnp.max(jnp.abs(block), axis=0, keepdims=True), 1e-30)
            sdst[i : i + 1, :] = top * (1.0 / 32767.0)
            qdst[i] = jnp.round(block * (32767.0 / top)).astype(jnp.int32).astype(jnp.int16)

    starts = [place_of_slot(i) for i in range(slots)]

    def panels():
        load_w.wait()
        hop = []
        for c in cols:
            encode(c, q.at[c], s.at[c])
            hop += to_cols(lambda c: s.at[c], rs.at[me], [c]) + to_cols(lambda c: q.at[c], rq.at[me], [c])
        encode(me, rq.at[me], rs.at[me])
        yield
        for copy in hop:
            copy.wait_recv()
        at_slot = lax.broadcasted_iota(jnp.int32, sels.shape, 0)
        for k in range(PIVOTS):
            slot = jnp.minimum(ranks[k], slots - 1)
            selq[k] = rq[owners[k], slot]
            picked = jnp.where(at_slot == slot, rs[owners[k]], 0.0)
            sels[k : k + 1, :] = jnp.sum(picked, axis=0, keepdims=True)
        beside = me + 1 - 2 * lax.rem(me, 2)
        ahead, behind = lax.rem(me + 2, COLDEV), lax.rem(me + 6, COLDEV)
        beside_ahead, beside_behind = lax.rem(beside + 2, COLDEV), lax.rem(beside + 6, COLDEV)
        across = net.remote(selq, qv.at[me], {"col": beside})
        first = [net.remote(selq, qv.at[me], {"col": c}) for c in (ahead, behind)]
        scales = to_cols(lambda c: sels, sv.at[me])
        keep = [net.own(selq, qv.at[me]), net.own(sels, sv.at[me])]
        yield
        across.wait_recv()
        second = [net.remote(qv.at[beside], qv.at[beside], {"col": c}) for c in (ahead, behind)]
        yield

        def pass_on(landed, from_behind, from_ahead):
            for copy in landed:
                copy.wait_recv()
            low, high = qv.at[from_behind, pl.ds(0, 4)], qv.at[from_ahead, pl.ds(4, 4)]
            return [net.remote(low, low, {"col": ahead}), net.remote(high, high, {"col": behind})]

        last = pass_on(first, behind, ahead)
        yield
        last += pass_on(second, beside_behind, beside_ahead)
        yield
        for copy in keep:
            copy.wait()
        for copy in last + scales:
            copy.wait_recv()
        yield

    def by_tile(values):
        at = lax.broadcasted_iota(jnp.int32, (rows, 1), 0) // BLOCK
        column = jnp.full((rows, 1), values[0], jnp.float32)
        for t in range(1, len(values)):
            column = jnp.where(at == t, values[t], column)
        return column

    def eliminate():
        load_d.wait()
        panels = [
            (qv[:, k].astype(jnp.int32).astype(jnp.float32) * sv[:, k : k + 1, :]).reshape(rows, BLOCK)
            for k in range(PIVOTS)
        ]
        for k in range(PIVOTS):
            errors = dot(jnp.concatenate(split(panels[k]), axis=1), jnp.concatenate([dv[k], dv[k]], axis=0))
            errors = errors * by_tile([prune[t, k].astype(jnp.float32) for t in range(rows // BLOCK)])
            hi, lo = split(errors)
            ev[k, :, :BLOCK] = hi
            ev[k, :, BLOCK:] = lo
            both = jnp.concatenate([hi, lo], axis=1)
            for n in range(k + 1, PIVOTS, 2):
                ends = list(range(n, min(n + 2, PIVOTS)))
                block = jnp.concatenate(
                    [jnp.concatenate([pv[e, g, k] for g in (0, 2, 1, 3)], axis=0) for e in ends], axis=1
                )
                new = dot(both, jnp.concatenate([block, block], axis=0))
                for i, e in enumerate(ends):
                    panels[e] = panels[e] - new[:, i * BLOCK : (i + 1) * BLOCK]
            yield

    def step_of(block):
        step = jnp.int32(PIVOTS)
        for k in range(PIVOTS):
            step = jnp.where((owners[k] == me) & (place(k) == block), k, step)
        return step

    def add(distances, last):
        pivots = [lax.rem(row.z + p + Z, Z) for p in distances]
        errors = jnp.concatenate([ev[j] for j in pivots], axis=1)
        per = SPAN // BLOCK

        @pl.loop(0, blocks_dev // per)
        def _(i):
            columns = pl.ds(pl.multiple_of(i * SPAN, SPAN), SPAN)
            steps = [step_of(i * per + b) for b in range(per)]
            parts = []
            for j in pivots:
                part = fo[pl.ds(4 * j, 4), :, columns].reshape(BLOCK, SPAN)
                used = [
                    jnp.full((BLOCK, BLOCK), jnp.where(j < step, 1.0, 0.0), jnp.float32).astype(f.dtype) for step in steps
                ]
                part = part * jnp.concatenate(used, axis=1)
                parts += [part, part]
            new = dot(errors, jnp.concatenate(parts, axis=0))
            for b, step in enumerate(steps):
                block = wv[i * per + b] - new[:, b * BLOCK : (b + 1) * BLOCK]
                if last:
                    kept = []
                    for t in range(rows // BLOCK):
                        pruned = prune[t, jnp.minimum(step, PIVOTS - 1)].astype(jnp.float32)
                        kept.append(jnp.where(step < PIVOTS, 1.0 - pruned, 1.0))
                    wv[i * per + b] = block * by_tile(kept)
                else:
                    wv[i * per + b] = block

    def update():
        for n, distances in enumerate(BATCHES):
            for d in sorted({abs(p) for p in distances}):
                for landed in given[d]:
                    landed()
            add(distances, n == len(BATCHES) - 1)
            yield
        stores = []
        for b in range(blocks_dev):
            pltpu.make_async_copy(wv.at[b], out.at[:, pl.ds(b * BLOCK, BLOCK)], local.at[15]).start()
        pltpu.make_async_copy(wv, wv, local.at[15]).wait()
        yield

    streams = {"P": pivot_columns, "F": factor, "W": panels, "R": eliminate, "U": update}
    streams = {name: stream() for name, stream in streams.items()}
    for name in ORDER:
        next(streams[name], None)
    for stream in streams.values():
        for _ in stream:
            pass
    net.finish()


def comm(slots, pivot_order, prune, w, f, d):
    (rows, width), frows = w.shape, f.shape[0]
    chunks, depth = rows // CHUNK, PIVOTS * BLOCK
    q = pltpu.VMEM((chunks, PIVOTS, CHUNK, BLOCK), jnp.int16)
    s = pltpu.VMEM((chunks, PIVOTS, BLOCK), jnp.float32)
    sent_q = pltpu.VMEM((COLDEV, slots, CHUNK, BLOCK), jnp.int16)
    sent_s = pltpu.VMEM((COLDEV, PIVOTS, BLOCK), jnp.float32)
    columns = pltpu.VMEM((PIVOTS, frows, BLOCK), f.dtype)
    return pl.pallas_call(
        functools.partial(comm_kernel, slots),
        in_specs=[SM, SM, ANY, ANY, ANY],
        out_specs=ANY,
        out_shape=jax.ShapeDtypeStruct(w.shape, w.dtype),
        scratch_shapes=[
            pltpu.VMEM((width // BLOCK, rows, BLOCK), w.dtype),
            pltpu.VMEM((width // BLOCK, frows, BLOCK), f.dtype),
            pltpu.VMEM(d.shape, d.dtype),
            columns,
            columns,
            pltpu.VMEM((frows, BLOCK), f.dtype),
            pltpu.VMEM((PIVOTS, 4, Z, frows, BLOCK), f.dtype),
            sent_q,
            sent_s,
            sent_q,
            sent_s,
            pltpu.VMEM((PIVOTS, CHUNK, BLOCK), jnp.int16),
            pltpu.VMEM((PIVOTS, BLOCK), jnp.float32),
            q,
            s,
            pltpu.VMEM((PIVOTS, rows, 2 * BLOCK), jnp.bfloat16),
            pltpu.VMEM((ROWDEV, frows, width), f.dtype),
            pltpu.SemaphoreType.DMA((COPIES,)),
            pltpu.SemaphoreType.DMA((COPIES,)),
            pltpu.SemaphoreType.DMA((16,)),
        ],
        compiler_params=pltpu.CompilerParams(collective_id=0 if slots < PIVOTS else 1, has_side_effects=True, vmem_limit_bytes=VMEM),
        name="comm",
    )(pivot_order, prune, w, f, d)


SLOTS = 4


def shards(weights, factor_rows, diag_inverse, prune_tiles, pivot_order):
    owners = pivot_order // (weights.shape[1] // BLOCK)
    pairs = jnp.sum((owners[:, None] == owners[None, :]).astype(jnp.int32))
    return lax.cond(
        pairs < (SLOTS + 1) ** 2 + PIVOTS - SLOTS - 1,
        functools.partial(comm, SLOTS),
        functools.partial(comm, PIVOTS),
        pivot_order,
        prune_tiles,
        weights,
        factor_rows,
        diag_inverse,
    )


def solution(mesh):
    return jax.shard_map(
        shards,
        mesh=mesh,
        in_specs=(P("row", "col"), P("row", "col"), P(), P("row", None), P()),
        out_specs=P("row", "col"),
        check_vma=False,
    )
```

```python
import functools

import jax
import jax.numpy as jnp
from jax import lax
from jax.experimental import pallas as pl
from jax.experimental.pallas import tpu as pltpu
from jax.sharding import PartitionSpec as P

BLOCK = 128
PIVOTS = 8
COLDEV = 8
ROWDEV = 32
Z = 8
CHUNK = 64
VMEM = 58 * 2**20
MESH = pl.DeviceIdType.MESH
ANY = pl.BlockSpec(memory_space=pl.ANY)
VM = pl.BlockSpec(memory_space=pltpu.VMEM)
SM = pl.BlockSpec(memory_space=pltpu.SMEM)


def once(copy):
    return [(None, copy)]


def each(cases, act):
    for when, copy in cases:
        if when is None:
            act(copy)
        else:
            pl.when(when)(lambda copy=copy: act(copy))


class Net:
    def __init__(self, send, recv, local):
        self.send, self.recv, self.local = send, recv, local
        self.sends = self.recvs = self.own_count = 0
        self.sent = []

    def new_send(self):
        self.sends += 1
        return self.sends - 1

    def new_recv(self, count=1):
        self.recvs += count
        return self.recvs - count

    def make(self, out, land, src, dst, device):
        return pltpu.make_async_remote_copy(
            src_ref=src,
            dst_ref=dst,
            send_sem=self.send.at[out],
            recv_sem=self.recv.at[land],
            device_id=device,
            device_id_type=MESH,
        )

    def here(self, out, land, ref):
        return self.make(out, land, ref, ref, {"row": lax.axis_index("row")})

    def some(self, sends, lands, land=None, out=None):
        land = self.new_recv() if land is None else land
        group, out = out is not None, self.new_send() if out is None else out
        cases = [(when, self.make(out, land, src, dst, device)) for when, src, dst, device in sends]
        each(cases, lambda copy: copy.start())
        if not group:
            self.sent.append(cases)
        return lambda: self.take(lands, land)

    def take(self, lands, land):
        each([(when, self.here(0, land, ref)) for when, ref in lands], lambda copy: copy.wait_recv())

    def remote(self, src, dst, device):
        copy = self.make(self.new_send(), self.new_recv(), src, dst, device)
        copy.start()
        self.sent.append(once(copy))
        return copy

    def group(self, copies, total):
        out, land = self.new_send(), self.new_recv()
        for src, dst, device in copies:
            self.make(out, land, src, dst, device).start()
        both = self.here(out, land, total)
        self.sent.append(once(both))
        return both

    def own(self, src, dst):
        copy = pltpu.make_async_copy(src, dst, self.local.at[self.own_count])
        self.own_count += 1
        copy.start()
        return copy

    def blocks(self, src, dst):
        sem = self.local.at[self.own_count]
        self.own_count += 1
        for b in range(dst.shape[0]):
            pltpu.make_async_copy(src.at[:, pl.ds(b * BLOCK, BLOCK)], dst.at[b], sem).start()
        return pltpu.make_async_copy(dst, dst, sem)

    def finish(self):
        for cases in self.sent:
            each(cases, lambda copy: copy.wait_send())


class Row:
    def __init__(self):
        r = lax.axis_index("row")
        core, xlo = lax.rem(r, 2), lax.rem(r // 2, 2)
        self.me, self.core, self.z = r, core, r // 4
        self.group = 2 * core + xlo
        self.sibling = r + 1 - 2 * core
        self.partner = r + 2 - 4 * xlo
        self.across = self.sibling + self.partner - r
        self.up, self.down = self.along(r, 1), self.along(r, -1)

    def along(self, base, steps):
        return lax.rem(base + 4 * steps + ROWDEV, ROWDEV)


def row_gather(net, row, out, mine, given):
    group = net.new_send()
    lands = [net.new_recv() for _ in range(5)]

    def shard(origin, device, arriving, view=lambda ref: ref, src=None, land=None):
        src = out.at[origin] if src is None else src
        sends = [(None, view(src), view(out.at[origin]), {"row": device})]
        return net.some(sends, [(None, view(out.at[arriving]))], land, group)

    def give(distance, origin, src=None):
        shard(origin, row.sibling, origin, src=src, land=lands[distance])

    def launch(base, step, src=None):
        up, down = row.along(base, -step), row.along(base, step)
        views = [lambda ref: ref] * 2 if step < 3 else [lambda ref, h=h: ref.at[pl.ds(16 * h, 16), :] for h in (0, 1)]
        return [
            shard(up, row.up, row.along(base, -step - 1), views[0], src),
            shard(down, row.down, row.along(base, step + 1), views[1], src),
        ]

    net.sent.append(once(net.here(group, 0, out.at[pl.ds(0, 1 + 14 + 16)])))
    for distance, land in enumerate(lands):
        shards = out.at[pl.ds(0, 2 if distance in (0, 4) else 4)]
        given[distance] = lambda shards=shards, land=land: net.take([(None, shards)], land)

    first = shard(row.me, row.partner, row.partner, src=mine)
    flight = [launch(row.me, 0, mine), None]
    give(0, row.me, mine)
    yield
    first()
    flight[1] = launch(row.partner, 0)
    give(0, row.partner)
    yield
    for step in range(4):
        for chain, base in ((0, row.me), (1, row.partner)):
            for landed in flight[chain]:
                landed()
            if step < 3:
                flight[chain] = launch(base, step + 1)
                give(step + 1, row.along(base, -step - 1))
                give(step + 1, row.along(base, step + 1))
            else:
                give(4, row.along(base, 4))
            yield


def split(x):
    hi = x.astype(jnp.bfloat16)
    return hi, (x - hi.astype(jnp.float32)).astype(jnp.bfloat16)


def dot(a, b):
    return jnp.dot(a, b, preferred_element_type=jnp.float32)


SENDS, RECVS = 36, 58
ORDER = "PFWPFFPWFFWPWFPFWPFWRRRRRRRRFFUFFUU"
BATCHES = ((0, -1, 1, -2, 2), (-3, 3, 4))
SPAN = 1024


def comm_kernel(
    slots, piv, prune, w, f, d, out,
    wv, fv, dv, fpv, r1, sel1, pv, q, s, rq, rs, selq, sels, qv, sv, ev, fo, send, recv, local,
):
    me = lax.axis_index("col")
    row = Row()
    rows = w.shape[0]
    blocks_dev = f.shape[1] // BLOCK
    cols = [lax.rem(me + d, COLDEV) for d in (2, 6, 1, 7, 4, 3, 5)]
    planes = [1, -1, 2, -2, 3, -3, 4]
    net = Net(send, recv, local)

    load_f, load_w, load_d = net.blocks(f, fv), net.blocks(w, wv), net.own(d, dv)
    barrier = pltpu.get_barrier_semaphore()
    for c in cols:
        pl.semaphore_signal(barrier, inc=1, device_id={"col": c}, device_id_type=MESH)
    for n in [row.sibling, row.partner] + [row.along(row.me, p) for p in planes]:
        pl.semaphore_signal(barrier, inc=1, device_id={"row": n}, device_id_type=MESH)

    base = net.new_recv(PIVOTS)

    def owners_of(k):
        return piv[k] // blocks_dev

    def place(k):
        return lax.rem(piv[k], blocks_dev)

    given = {}

    def factor():
        keep = net.own(f, fo.at[row.me])
        gather = row_gather(net, row, fo, f, given)
        next(gather)
        yield
        keep.wait()
        yield from gather

    def pivot_columns():
        load_f.wait()
        for k in range(1, PIVOTS):
            fpv[k] = fv[place(k)]
        pl.semaphore_wait(barrier, COLDEV - 1 + 9)
        hop = [net.some([(c > row.z, fpv.at[c], r1.at[me], {"col": c})], [(me > row.z, r1.at[me])]) for c in cols]
        yield
        for landed in hop:
            landed()

        @pl.when(me > row.z)
        def _():
            r1[me] = fpv[me]
            sel1[...] = r1[owners_of(me)]
            pv[me, row.group, row.z] = sel1[...]

        hop = []
        for p in planes:
            origin = row.along(row.me, -p) // 4
            hop.append(
                net.some(
                    [(me > row.z, sel1, pv.at[me, row.group, row.z], {"row": row.along(row.me, p)})],
                    [(me > origin, sel1)],
                )
            )
        yield
        for landed in hop:
            landed()
        for c in cols:
            sends = []
            for k in range(1, PIVOTS):
                above = pv.at[k, row.group, pl.ds(0, k)]
                sends.append((me == k, above, above, {"col": c}))
            net.some(sends, [], base + me)
        yield
        above = [(k, pv.at[k, row.group, pl.ds(0, k)]) for k in range(1, PIVOTS)]
        for k, ref in above:
            net.take([(me != k, ref)], base + k)
        across = net.group([(ref, ref, {"row": row.partner}) for _, ref in above], pv.at[0, :, pl.ds(0, PIVOTS - 1)])
        yield
        across.wait_recv()
        above = [pv.at[k, pl.ds(2 * row.core, 2), pl.ds(0, k)] for k in range(1, PIVOTS)]
        last = net.group([(ref, ref, {"row": row.sibling}) for ref in above], pv.at[0:2, :, pl.ds(0, PIVOTS - 1)])
        yield
        last.wait_recv()
        yield

    owners = [piv[k] // blocks_dev for k in range(PIVOTS)]
    ranks = [sum(((owners[i] == owners[k]).astype(jnp.int32) for i in range(k)), jnp.int32(0)) for k in range(PIVOTS)]

    def place_of_slot(i):
        start = jnp.int32(0)
        for k in range(PIVOTS):
            start = jnp.where((owners[k] == me) & (ranks[k] == i), place(k), start)
        return start

    def encode(chunk, qdst, sdst):
        rows_c = pl.ds(pl.multiple_of(chunk * CHUNK, CHUNK), CHUNK)
        for i in range(slots):
            block = wv[starts[i], rows_c]
            top = jnp.maximum(jnp.max(jnp.abs(block), axis=0, keepdims=True), 1e-30)
            sdst[i : i + 1, :] = top * (1.0 / 32767.0)
            qdst[i] = jnp.round(block * (32767.0 / top)).astype(jnp.int32).astype(jnp.int16)

    starts = [place_of_slot(i) for i in range(slots)]

    def panels():
        load_w.wait()
        outs, lands = [net.new_send() for _ in range(2)], [net.new_recv() for _ in range(2)]
        pairs = (q, rq), (s, rs)
        for c in cols:
            encode(c, q.at[c], s.at[c])
            for out_sem, land, (here, there) in zip(outs, lands, pairs):
                net.some([(None, here.at[c], there.at[me], {"col": c})], [], land, out_sem)
        hop = [net.here(o, n, here.at[pl.ds(0, COLDEV - 1)]) for o, n, (here, _) in zip(outs, lands, pairs)]
        net.sent += [once(copy) for copy in hop]
        encode(me, rq.at[me], rs.at[me])
        yield
        for copy in hop:
            copy.wait_recv()
        at_slot = lax.broadcasted_iota(jnp.int32, sels.shape, 0)
        for k in range(PIVOTS):
            slot = jnp.minimum(ranks[k], slots - 1)
            selq[k] = rq[owners[k], slot]
            picked = jnp.where(at_slot == slot, rs[owners[k]], 0.0)
            sels[k : k + 1, :] = jnp.sum(picked, axis=0, keepdims=True)
        beside = me + 1 - 2 * lax.rem(me, 2)
        ahead, behind = lax.rem(me + 2, COLDEV), lax.rem(me + 6, COLDEV)
        beside_ahead, beside_behind = lax.rem(beside + 2, COLDEV), lax.rem(beside + 6, COLDEV)
        across = net.remote(selq, qv.at[me], {"col": beside})
        first = [net.remote(selq, qv.at[me], {"col": c}) for c in (ahead, behind)]
        scales = [net.group([(sels, sv.at[me], {"col": c}) for c in cols], sv.at[pl.ds(0, COLDEV - 1)])]
        keep = [net.own(selq, qv.at[me]), net.own(sels, sv.at[me])]
        yield
        across.wait_recv()
        second = [net.remote(qv.at[beside], qv.at[beside], {"col": c}) for c in (ahead, behind)]
        yield

        def pass_on(landed, from_behind, from_ahead):
            for copy in landed:
                copy.wait_recv()
            low, high = qv.at[from_behind, pl.ds(0, 4)], qv.at[from_ahead, pl.ds(4, 4)]
            return [net.remote(low, low, {"col": ahead}), net.remote(high, high, {"col": behind})]

        last = pass_on(first, behind, ahead)
        yield
        last += pass_on(second, beside_behind, beside_ahead)
        yield
        for copy in keep:
            copy.wait()
        for copy in last + scales:
            copy.wait_recv()
        yield

    def by_tile(values):
        at = lax.broadcasted_iota(jnp.int32, (rows, 1), 0) // BLOCK
        column = jnp.full((rows, 1), values[0], jnp.float32)
        for t in range(1, len(values)):
            column = jnp.where(at == t, values[t], column)
        return column

    def eliminate():
        load_d.wait()
        panels = [
            (qv[:, k].astype(jnp.int32).astype(jnp.float32) * sv[:, k : k + 1, :]).reshape(rows, BLOCK)
            for k in range(PIVOTS)
        ]
        for k in range(PIVOTS):
            errors = dot(jnp.concatenate(split(panels[k]), axis=1), jnp.concatenate([dv[k], dv[k]], axis=0))
            errors = errors * by_tile([prune[t, k].astype(jnp.float32) for t in range(rows // BLOCK)])
            hi, lo = split(errors)
            ev[k, :, :BLOCK] = hi
            ev[k, :, BLOCK:] = lo
            both = jnp.concatenate([hi, lo], axis=1)
            for n in range(k + 1, PIVOTS, 2):
                ends = list(range(n, min(n + 2, PIVOTS)))
                block = jnp.concatenate(
                    [jnp.concatenate([pv[e, g, k] for g in (0, 2, 1, 3)], axis=0) for e in ends], axis=1
                )
                new = dot(both, jnp.concatenate([block, block], axis=0))
                for i, e in enumerate(ends):
                    panels[e] = panels[e] - new[:, i * BLOCK : (i + 1) * BLOCK]
            yield

    def step_of(block):
        step = jnp.int32(PIVOTS)
        for k in range(PIVOTS):
            step = jnp.where((owners[k] == me) & (place(k) == block), k, step)
        return step

    def add(distances, last):
        pivots = [lax.rem(row.z + p + Z, Z) for p in distances]
        errors = jnp.concatenate([ev[j] for j in pivots], axis=1)
        per = SPAN // BLOCK

        @pl.loop(0, blocks_dev // per)
        def _(i):
            columns = pl.ds(pl.multiple_of(i * SPAN, SPAN), SPAN)
            steps = [step_of(i * per + b) for b in range(per)]
            parts = []
            for j in pivots:
                part = fo[pl.ds(4 * j, 4), :, columns].reshape(BLOCK, SPAN)
                used = [
                    jnp.full((BLOCK, BLOCK), jnp.where(j < step, 1.0, 0.0), jnp.float32).astype(f.dtype) for step in steps
                ]
                part = part * jnp.concatenate(used, axis=1)
                parts += [part, part]
            new = dot(errors, jnp.concatenate(parts, axis=0))
            for b, step in enumerate(steps):
                block = wv[i * per + b] - new[:, b * BLOCK : (b + 1) * BLOCK]
                if last:
                    kept = []
                    for t in range(rows // BLOCK):
                        pruned = prune[t, jnp.minimum(step, PIVOTS - 1)].astype(jnp.float32)
                        kept.append(jnp.where(step < PIVOTS, 1.0 - pruned, 1.0))
                    wv[i * per + b] = block * by_tile(kept)
                else:
                    wv[i * per + b] = block
            if last:
                for b in range(per):
                    columns = pl.ds(pl.multiple_of((i * per + b) * BLOCK, BLOCK), BLOCK)
                    pltpu.make_async_copy(wv.at[i * per + b], out.at[:, columns], local.at[15]).start()

    def update():
        for n, distances in enumerate(BATCHES):
            for d in sorted({abs(p) for p in distances}):
                given[d]()
            add(distances, n == len(BATCHES) - 1)
            yield
        pltpu.make_async_copy(wv, wv, local.at[15]).wait()
        yield

    streams = {"P": pivot_columns, "F": factor, "W": panels, "R": eliminate, "U": update}
    streams = {name: stream() for name, stream in streams.items()}
    for name in ORDER:
        next(streams[name], None)
    for stream in streams.values():
        for _ in stream:
            pass
    assert (net.sends, net.recvs) == (SENDS, RECVS), (net.sends, net.recvs)
    net.finish()


def comm(slots, pivot_order, prune, w, f, d):
    (rows, width), frows = w.shape, f.shape[0]
    chunks, depth = rows // CHUNK, PIVOTS * BLOCK
    q = pltpu.VMEM((chunks, PIVOTS, CHUNK, BLOCK), jnp.int16)
    s = pltpu.VMEM((chunks, PIVOTS, BLOCK), jnp.float32)
    sent_q = pltpu.VMEM((COLDEV, slots, CHUNK, BLOCK), jnp.int16)
    sent_s = pltpu.VMEM((COLDEV, PIVOTS, BLOCK), jnp.float32)
    columns = pltpu.VMEM((PIVOTS, frows, BLOCK), f.dtype)
    return pl.pallas_call(
        functools.partial(comm_kernel, slots),
        in_specs=[SM, SM, ANY, ANY, ANY],
        out_specs=ANY,
        out_shape=jax.ShapeDtypeStruct(w.shape, w.dtype),
        scratch_shapes=[
            pltpu.VMEM((width // BLOCK, rows, BLOCK), w.dtype),
            pltpu.VMEM((width // BLOCK, frows, BLOCK), f.dtype),
            pltpu.VMEM(d.shape, d.dtype),
            columns,
            columns,
            pltpu.VMEM((frows, BLOCK), f.dtype),
            pltpu.VMEM((PIVOTS, 4, Z, frows, BLOCK), f.dtype),
            sent_q,
            sent_s,
            sent_q,
            sent_s,
            pltpu.VMEM((PIVOTS, CHUNK, BLOCK), jnp.int16),
            pltpu.VMEM((PIVOTS, BLOCK), jnp.float32),
            q,
            s,
            pltpu.VMEM((PIVOTS, rows, 2 * BLOCK), jnp.bfloat16),
            pltpu.VMEM((ROWDEV, frows, width), f.dtype),
            pltpu.SemaphoreType.DMA((SENDS,)),
            pltpu.SemaphoreType.DMA((RECVS,)),
            pltpu.SemaphoreType.DMA((16,)),
        ],
        compiler_params=pltpu.CompilerParams(collective_id=0 if slots < PIVOTS else 1, has_side_effects=True, vmem_limit_bytes=VMEM),
        name="comm",
    )(pivot_order, prune, w, f, d)


SLOTS = 4


def shards(weights, factor_rows, diag_inverse, prune_tiles, pivot_order):
    blocks_dev = weights.shape[1] // BLOCK
    pairs = jnp.sum(((pivot_order[:, None] ^ pivot_order[None, :]) < blocks_dev).astype(jnp.int32))
    return lax.cond(
        pairs < (SLOTS + 1) ** 2 + PIVOTS - SLOTS - 1,
        functools.partial(comm, SLOTS),
        functools.partial(comm, PIVOTS),
        pivot_order,
        prune_tiles,
        weights,
        factor_rows,
        diag_inverse,
    )


def solution(mesh):
    return jax.shard_map(
        shards,
        mesh=mesh,
        in_specs=(P("row", "col"), P("row", "col"), P(), P("row", None), P()),
        out_specs=P("row", "col"),
        check_vma=False,
    )
```

```python
import functools

import jax
import jax.numpy as jnp
from jax import lax
from jax.experimental import pallas as pl
from jax.experimental.pallas import tpu as pltpu
from jax.sharding import PartitionSpec as P

BLOCK = 128
PIVOTS = 8
COLDEV = 8
ROWDEV = 32
Z = 8
CHUNK = 64
VMEM = 58 * 2**20
MESH = pl.DeviceIdType.MESH
ANY = pl.BlockSpec(memory_space=pl.ANY)
VM = pl.BlockSpec(memory_space=pltpu.VMEM)
SM = pl.BlockSpec(memory_space=pltpu.SMEM)


def once(copy):
    return [(None, copy)]


def each(cases, act):
    for when, copy in cases:
        if when is None:
            act(copy)
        else:
            pl.when(when)(lambda copy=copy: act(copy))


class Net:
    def __init__(self, send, recv, local):
        self.send, self.recv, self.local = send, recv, local
        self.sends = self.recvs = self.own_count = 0
        self.sent = []

    def new_send(self):
        self.sends += 1
        return self.sends - 1

    def new_recv(self, count=1):
        self.recvs += count
        return self.recvs - count

    def make(self, out, land, src, dst, device):
        return pltpu.make_async_remote_copy(
            src_ref=src,
            dst_ref=dst,
            send_sem=self.send.at[out],
            recv_sem=self.recv.at[land],
            device_id=device,
            device_id_type=MESH,
        )

    def here(self, out, land, ref):
        return self.make(out, land, ref, ref, {"row": lax.axis_index("row")})

    def some(self, sends, lands, land=None, out=None):
        land = self.new_recv() if land is None else land
        group, out = out is not None, self.new_send() if out is None else out
        cases = [(when, self.make(out, land, src, dst, device)) for when, src, dst, device in sends]
        each(cases, lambda copy: copy.start())
        if not group:
            self.sent.append(cases)
        return lambda: self.take(lands, land)

    def take(self, lands, land):
        each([(when, self.here(0, land, ref)) for when, ref in lands], lambda copy: copy.wait_recv())

    def remote(self, src, dst, device):
        copy = self.make(self.new_send(), self.new_recv(), src, dst, device)
        copy.start()
        self.sent.append(once(copy))
        return copy

    def group(self, copies, total):
        out, land = self.new_send(), self.new_recv()
        for src, dst, device in copies:
            self.make(out, land, src, dst, device).start()
        both = self.here(out, land, total)
        self.sent.append(once(both))
        return both

    def own(self, src, dst):
        copy = pltpu.make_async_copy(src, dst, self.local.at[self.own_count])
        self.own_count += 1
        copy.start()
        return copy

    def blocks(self, src, dst):
        sem = self.local.at[self.own_count]
        self.own_count += 1
        for b in range(dst.shape[0]):
            pltpu.make_async_copy(src.at[:, pl.ds(b * BLOCK, BLOCK)], dst.at[b], sem).start()
        return pltpu.make_async_copy(dst, dst, sem)

    def finish(self):
        for cases in self.sent:
            each(cases, lambda copy: copy.wait_send())


class Row:
    def __init__(self):
        r = lax.axis_index("row")
        core, xlo = lax.rem(r, 2), lax.rem(r // 2, 2)
        self.me, self.core, self.z = r, core, r // 4
        self.group = 2 * core + xlo
        self.sibling = r + 1 - 2 * core
        self.partner = r + 2 - 4 * xlo
        self.across = self.sibling + self.partner - r
        self.up, self.down = self.along(r, 1), self.along(r, -1)

    def along(self, base, steps):
        return lax.rem(base + 4 * steps + ROWDEV, ROWDEV)


def row_gather(net, row, out, mine, given):
    group = net.new_send()
    lands = [net.new_recv() for _ in range(5)]

    def shard(origin, device, arriving, view=lambda ref: ref, src=None, land=None):
        src = out.at[origin] if src is None else src
        sends = [(None, view(src), view(out.at[origin]), {"row": device})]
        return net.some(sends, [(None, view(out.at[arriving]))], land, group)

    def give(distance, origin, src=None):
        shard(origin, row.sibling, origin, src=src, land=lands[distance])

    def launch(base, step, src=None):
        up, down = row.along(base, -step), row.along(base, step)
        views = [lambda ref: ref] * 2 if step < 3 else [lambda ref, h=h: ref.at[pl.ds(16 * h, 16), :] for h in (0, 1)]
        return [
            shard(up, row.up, row.along(base, -step - 1), views[0], src),
            shard(down, row.down, row.along(base, step + 1), views[1], src),
        ]

    net.sent.append(once(net.here(group, 0, out.at[pl.ds(0, 1 + 14 + 16)])))
    for distance, land in enumerate(lands):
        shards = out.at[pl.ds(0, 2 if distance in (0, 4) else 4)]
        given[distance] = lambda shards=shards, land=land: net.take([(None, shards)], land)

    first = shard(row.me, row.partner, row.partner, src=mine)
    flight = [launch(row.me, 0, mine), None]
    give(0, row.me, mine)
    yield
    first()
    flight[1] = launch(row.partner, 0)
    give(0, row.partner)
    yield
    for step in range(4):
        for chain, base in ((0, row.me), (1, row.partner)):
            for landed in flight[chain]:
                landed()
            if step < 3:
                flight[chain] = launch(base, step + 1)
                give(step + 1, row.along(base, -step - 1))
                give(step + 1, row.along(base, step + 1))
            else:
                give(4, row.along(base, 4))
            yield


def split(x):
    hi = x.astype(jnp.bfloat16)
    return hi, (x - hi.astype(jnp.float32)).astype(jnp.bfloat16)


def dot(a, b):
    return jnp.dot(a, b, preferred_element_type=jnp.float32)


SENDS, RECVS = 36, 58
ORDER = "PFWPFFPWFFWFPWFPWFPWRRRRRRRRFFUFUU"
BATCHES = ((0, -1, 1, -2, 2), (-3, 3, 4))
SPAN = 1024


def comm_kernel(
    slots, piv, prune, w, f, d, out,
    wv, fv, dv, fpv, r1, sel1, pv, q, s, rq, rs, selq, sels, qv, sv, ev, fo, send, recv, local,
):
    me = lax.axis_index("col")
    row = Row()
    rows = w.shape[0]
    blocks_dev = f.shape[1] // BLOCK
    cols = [lax.rem(me + d, COLDEV) for d in (2, 6, 1, 7, 4, 3, 5)]
    planes = [1, -1, 2, -2, 3, -3, 4]
    net = Net(send, recv, local)

    load_f, load_w, load_d = net.blocks(f, fv), net.blocks(w, wv), net.own(d, dv)
    barrier = pltpu.get_barrier_semaphore()
    for c in cols:
        pl.semaphore_signal(barrier, inc=1, device_id={"col": c}, device_id_type=MESH)
    for n in [row.sibling, row.partner] + [row.along(row.me, p) for p in planes]:
        pl.semaphore_signal(barrier, inc=1, device_id={"row": n}, device_id_type=MESH)

    base = net.new_recv(PIVOTS)

    def owners_of(k):
        return piv[k] // blocks_dev

    def place(k):
        return lax.rem(piv[k], blocks_dev)

    given = {}

    def factor():
        keep = net.own(f, fo.at[row.me])
        gather = row_gather(net, row, fo, f, given)
        next(gather)
        yield
        keep.wait()
        yield from gather

    def pivot_columns():
        load_f.wait()
        for k in range(1, PIVOTS):
            fpv[k] = fv[place(k)]
        pl.semaphore_wait(barrier, COLDEV - 1 + 9)
        hop = [net.some([(c > row.z, fpv.at[c], r1.at[me], {"col": c})], [(me > row.z, r1.at[me])]) for c in cols]
        yield
        for landed in hop:
            landed()

        @pl.when(me > row.z)
        def _():
            r1[me] = fpv[me]
            sel1[...] = r1[owners_of(me)]
            pv[me, row.group, row.z] = sel1[...]

        hop = []
        for p in planes:
            origin = row.along(row.me, -p) // 4
            hop.append(
                net.some(
                    [(me > row.z, sel1, pv.at[me, row.group, row.z], {"row": row.along(row.me, p)})],
                    [(me > origin, sel1)],
                )
            )
        yield
        for landed in hop:
            landed()
        for c in cols:
            sends = []
            for k in range(1, PIVOTS):
                above = pv.at[k, row.group, pl.ds(0, k)]
                sends.append((me == k, above, above, {"col": c}))
            net.some(sends, [], base + me)
        yield
        above = [(k, pv.at[k, row.group, pl.ds(0, k)]) for k in range(1, PIVOTS)]
        for k, ref in above:
            net.take([(me != k, ref)], base + k)
        across = net.group([(ref, ref, {"row": row.partner}) for _, ref in above], pv.at[0, :, pl.ds(0, PIVOTS - 1)])
        yield
        across.wait_recv()
        above = [pv.at[k, pl.ds(2 * row.core, 2), pl.ds(0, k)] for k in range(1, PIVOTS)]
        last = net.group([(ref, ref, {"row": row.sibling}) for ref in above], pv.at[0:2, :, pl.ds(0, PIVOTS - 1)])
        yield
        last.wait_recv()
        yield

    owners = [piv[k] // blocks_dev for k in range(PIVOTS)]
    ranks = [sum(((owners[i] == owners[k]).astype(jnp.int32) for i in range(k)), jnp.int32(0)) for k in range(PIVOTS)]

    def place_of_slot(i):
        start = jnp.int32(0)
        for k in range(PIVOTS):
            start = jnp.where((owners[k] == me) & (ranks[k] == i), place(k), start)
        return start

    def encode(chunk, qdst, sdst):
        rows_c = pl.ds(pl.multiple_of(chunk * CHUNK, CHUNK), CHUNK)
        for i in range(slots):
            block = wv[starts[i], rows_c]
            top = jnp.maximum(jnp.max(jnp.abs(block), axis=0, keepdims=True), 1e-30)
            sdst[i : i + 1, :] = top * (1.0 / 32767.0)
            qdst[i] = jnp.round(block * (32767.0 / top)).astype(jnp.int32).astype(jnp.int16)

    starts = [place_of_slot(i) for i in range(slots)]

    def panels():
        load_w.wait()
        outs, lands = [net.new_send() for _ in range(2)], [net.new_recv() for _ in range(2)]
        pairs = (q, rq), (s, rs)
        for c in cols:
            encode(c, q.at[c], s.at[c])
            for out_sem, land, (here, there) in zip(outs, lands, pairs):
                net.some([(None, here.at[c], there.at[me], {"col": c})], [], land, out_sem)
        hop = [net.here(o, n, here.at[pl.ds(0, COLDEV - 1)]) for o, n, (here, _) in zip(outs, lands, pairs)]
        net.sent += [once(copy) for copy in hop]
        encode(me, rq.at[me], rs.at[me])
        yield
        for copy in hop:
            copy.wait_recv()
        at_slot = lax.broadcasted_iota(jnp.int32, sels.shape, 0)
        for k in range(PIVOTS):
            slot = jnp.minimum(ranks[k], slots - 1)
            selq[k] = rq[owners[k], slot]
            picked = jnp.where(at_slot == slot, rs[owners[k]], 0.0)
            sels[k : k + 1, :] = jnp.sum(picked, axis=0, keepdims=True)
        beside = me + 1 - 2 * lax.rem(me, 2)
        ahead, behind = lax.rem(me + 2, COLDEV), lax.rem(me + 6, COLDEV)
        beside_ahead, beside_behind = lax.rem(beside + 2, COLDEV), lax.rem(beside + 6, COLDEV)
        across = net.remote(selq, qv.at[me], {"col": beside})
        first = [net.remote(selq, qv.at[me], {"col": c}) for c in (ahead, behind)]
        scales = [net.group([(sels, sv.at[me], {"col": c}) for c in cols], sv.at[pl.ds(0, COLDEV - 1)])]
        keep = [net.own(selq, qv.at[me]), net.own(sels, sv.at[me])]
        yield
        across.wait_recv()
        second = [net.remote(qv.at[beside], qv.at[beside], {"col": c}) for c in (ahead, behind)]
        yield

        def pass_on(landed, from_behind, from_ahead):
            for copy in landed:
                copy.wait_recv()
            low, high = qv.at[from_behind, pl.ds(0, 4)], qv.at[from_ahead, pl.ds(4, 4)]
            return [net.remote(low, low, {"col": ahead}), net.remote(high, high, {"col": behind})]

        last = pass_on(first, behind, ahead)
        yield
        last += pass_on(second, beside_behind, beside_ahead)
        yield
        for copy in keep:
            copy.wait()
        for copy in last + scales:
            copy.wait_recv()
        yield

    def by_tile(values):
        at = lax.broadcasted_iota(jnp.int32, (rows, 1), 0) // BLOCK
        column = jnp.full((rows, 1), values[0], jnp.float32)
        for t in range(1, len(values)):
            column = jnp.where(at == t, values[t], column)
        return column

    def eliminate():
        load_d.wait()
        panels = [
            (qv[:, k].astype(jnp.int32).astype(jnp.float32) * sv[:, k : k + 1, :]).reshape(rows, BLOCK)
            for k in range(PIVOTS)
        ]
        for k in range(PIVOTS):
            errors = dot(jnp.concatenate(split(panels[k]), axis=1), jnp.concatenate([dv[k], dv[k]], axis=0))
            errors = errors * by_tile([prune[t, k].astype(jnp.float32) for t in range(rows // BLOCK)])
            hi, lo = split(errors)
            ev[k, :, :BLOCK] = hi
            ev[k, :, BLOCK:] = lo
            both = jnp.concatenate([hi, lo], axis=1)
            for n in range(k + 1, PIVOTS, 2):
                ends = list(range(n, min(n + 2, PIVOTS)))
                block = jnp.concatenate(
                    [jnp.concatenate([pv[e, g, k] for g in (0, 2, 1, 3)], axis=0) for e in ends], axis=1
                )
                new = dot(both, jnp.concatenate([block, block], axis=0))
                for i, e in enumerate(ends):
                    panels[e] = panels[e] - new[:, i * BLOCK : (i + 1) * BLOCK]
            yield

    def step_of(block):
        step = jnp.int32(PIVOTS)
        for k in range(PIVOTS):
            step = jnp.where((owners[k] == me) & (place(k) == block), k, step)
        return step

    def add(distances, last):
        pivots = [lax.rem(row.z + p + Z, Z) for p in distances]
        errors = jnp.concatenate([ev[j] for j in pivots], axis=1)
        per = SPAN // BLOCK

        @pl.loop(0, blocks_dev // per)
        def _(i):
            columns = pl.ds(pl.multiple_of(i * SPAN, SPAN), SPAN)
            steps = [step_of(i * per + b) for b in range(per)]
            parts = []
            for j in pivots:
                part = fo[pl.ds(4 * j, 4), :, columns].reshape(BLOCK, SPAN)
                used = [
                    jnp.full((BLOCK, BLOCK), jnp.where(j < step, 1.0, 0.0), jnp.float32).astype(f.dtype) for step in steps
                ]
                part = part * jnp.concatenate(used, axis=1)
                parts += [part, part]
            new = dot(errors, jnp.concatenate(parts, axis=0))
            for b, step in enumerate(steps):
                block = wv[i * per + b] - new[:, b * BLOCK : (b + 1) * BLOCK]
                if last:
                    kept = []
                    for t in range(rows // BLOCK):
                        pruned = prune[t, jnp.minimum(step, PIVOTS - 1)].astype(jnp.float32)
                        kept.append(jnp.where(step < PIVOTS, 1.0 - pruned, 1.0))
                    wv[i * per + b] = block * by_tile(kept)
                else:
                    wv[i * per + b] = block
            if last:
                for b in range(per):
                    columns = pl.ds(pl.multiple_of((i * per + b) * BLOCK, BLOCK), BLOCK)
                    pltpu.make_async_copy(wv.at[i * per + b], out.at[:, columns], local.at[15]).start()

    def update():
        for n, distances in enumerate(BATCHES):
            for d in sorted({abs(p) for p in distances}):
                given[d]()
            add(distances, n == len(BATCHES) - 1)
            yield
        pltpu.make_async_copy(wv, wv, local.at[15]).wait()
        yield

    streams = {"P": pivot_columns, "F": factor, "W": panels, "R": eliminate, "U": update}
    streams = {name: stream() for name, stream in streams.items()}
    for name in ORDER:
        next(streams[name], None)
    for stream in streams.values():
        for _ in stream:
            pass
    assert (net.sends, net.recvs) == (SENDS, RECVS), (net.sends, net.recvs)
    net.finish()


def comm(slots, pivot_order, prune, w, f, d):
    (rows, width), frows = w.shape, f.shape[0]
    chunks, depth = rows // CHUNK, PIVOTS * BLOCK
    q = pltpu.VMEM((chunks, PIVOTS, CHUNK, BLOCK), jnp.int16)
    s = pltpu.VMEM((chunks, PIVOTS, BLOCK), jnp.float32)
    sent_q = pltpu.VMEM((COLDEV, slots, CHUNK, BLOCK), jnp.int16)
    sent_s = pltpu.VMEM((COLDEV, PIVOTS, BLOCK), jnp.float32)
    columns = pltpu.VMEM((PIVOTS, frows, BLOCK), f.dtype)
    return pl.pallas_call(
        functools.partial(comm_kernel, slots),
        in_specs=[SM, SM, ANY, ANY, ANY],
        out_specs=ANY,
        out_shape=jax.ShapeDtypeStruct(w.shape, w.dtype),
        scratch_shapes=[
            pltpu.VMEM((width // BLOCK, rows, BLOCK), w.dtype),
            pltpu.VMEM((width // BLOCK, frows, BLOCK), f.dtype),
            pltpu.VMEM(d.shape, d.dtype),
            columns,
            columns,
            pltpu.VMEM((frows, BLOCK), f.dtype),
            pltpu.VMEM((PIVOTS, 4, Z, frows, BLOCK), f.dtype),
            sent_q,
            sent_s,
            sent_q,
            sent_s,
            pltpu.VMEM((PIVOTS, CHUNK, BLOCK), jnp.int16),
            pltpu.VMEM((PIVOTS, BLOCK), jnp.float32),
            q,
            s,
            pltpu.VMEM((PIVOTS, rows, 2 * BLOCK), jnp.bfloat16),
            pltpu.VMEM((ROWDEV, frows, width), f.dtype),
            pltpu.SemaphoreType.DMA((SENDS,)),
            pltpu.SemaphoreType.DMA((RECVS,)),
            pltpu.SemaphoreType.DMA((16,)),
        ],
        compiler_params=pltpu.CompilerParams(collective_id=0 if slots < PIVOTS else 1, has_side_effects=True, vmem_limit_bytes=VMEM),
        name="comm",
    )(pivot_order, prune, w, f, d)


SLOTS = 4


def shards(weights, factor_rows, diag_inverse, prune_tiles, pivot_order):
    blocks_dev = weights.shape[1] // BLOCK
    pairs = jnp.sum(((pivot_order[:, None] ^ pivot_order[None, :]) < blocks_dev).astype(jnp.int32))
    return lax.cond(
        pairs < (SLOTS + 1) ** 2 + PIVOTS - SLOTS - 1,
        functools.partial(comm, SLOTS),
        functools.partial(comm, PIVOTS),
        pivot_order,
        prune_tiles,
        weights,
        factor_rows,
        diag_inverse,
    )


def solution(mesh):
    return jax.shard_map(
        shards,
        mesh=mesh,
        in_specs=(P("row", "col"), P("row", "col"), P(), P("row", None), P()),
        out_specs=P("row", "col"),
        check_vma=False,
    )
```
